32 devices in a mesh: lon: 8 (over z, y), lat: 4 (over x, core).
Axes of the slice: x: 2, y: 2, z: 4, core: 2. Of those that a mesh axis runs over, the one named last changes fastest.
Arguments:
- tokens: bfloat16 [128, 256, 768], P('lat', 'lon'), may hold values from -6 to 6
- norm_gain: float32 [768], replicated, may hold values from 0.1 to 1.9
- inproj_weight: bfloat16 [768, 1152], P('lat')
- outproj_weight: bfloat16 [384, 768], P('lat'), may hold values from -0.3125 to 0.3125
- merge_gain: float32 [3072], replicated, may hold values from 0.1 to 1.9
- merge_weight: bfloat16 [3072, 768], P('lat'), may hold values from -0.109375 to 0.109375
- ocean_flags: int32 [8, 16], P('lat', 'lon'), may hold values 0 or 1
- fold_partner: int32 [256], P('lon'), may hold values from 0 to 255, as said below
Outputs:
- merged: bfloat16 [64, 128, 768], P('lat', 'lon')
The draws below stay inside these ranges and needn't reach their ends.
Inputs may be any that keep to these rules, and one draw needn't show every extreme that they name: `fold_partner`: the 32 entries c in [i*32, (i+1)*32) name each column of the block [(256 // 32 - 1 - i)*32, (256 // 32 - i)*32) once.
All inputs are finite; a program needn't handle non-finite values. No bound on the sum of `ocean_flags` on one device may be relied on, other than what follows from the above.
Results may differ from the reference program's by a relative error of at most 0.0063.
Values may be sent and summed in bfloat16 or wider, within the bound.
A program may use at most 64 MiB of HBM per device.

```python
import jax
import jax.numpy as jnp
from jax import lax

D = 768
HEADS = 12
HD = 32
DM = 768
WIN = 16
HALF = 8
W_DEV = 32
NLAT = 128
NLON = 256


def draw_inproj_weight(key, part):
    head_width = HEADS * HD
    drawn = jax.random.normal(key, (D, 3 * head_width), jnp.float32) * D ** (-0.5)
    return drawn.astype(jnp.bfloat16)


def draw_fold_partner(key, part):
    block_count = NLON // W_DEV
    sub_keys = jax.random.split(key, block_count)

    def shuffle(sub_key):
        return jax.random.permutation(sub_key, W_DEV).astype(jnp.int32)
    shuffled = jax.vmap(shuffle)(sub_keys)
    starts = (block_count - 1 - jnp.arange(block_count, dtype=jnp.int32)) * W_DEV
    return (shuffled + starts[:, None]).reshape(-1).astype(jnp.int32)


def touch_ends(entries, key, least, largest):
    index_at = [jax.random.randint(jax.random.fold_in(key, axis), (), 0, length) for axis, length in enumerate(entries.shape)]
    longest = entries.shape.index(max(entries.shape))
    neighbour = index_at[:longest] + [(index_at[longest] + 1) % entries.shape[longest]] + index_at[longest + 1:]
    return entries.at[tuple(index_at)].set(least).at[tuple(neighbour)].set(largest)


def steps_of(own_key, shape, shards, low, high):
    def one(position, blocks):
        steps = jax.random.uniform(jax.random.fold_in(jax.random.fold_in(own_key, 6), position), (blocks,), jnp.float32, low / len(shards), high / len(shards))
        return jnp.repeat(jnp.exp(steps), shape[position] // blocks).reshape((-1,) + (1,) * (len(shape) - position - 1))

    factor_of = one(*shards[0])
    for cut in shards[1:]:
        factor_of = factor_of * one(*cut)
    return factor_of


def scatter_about(own_key, shape, width, most, shards=(), held_as=jnp.bfloat16):
    values = width * jax.random.normal(own_key, shape, jnp.float32)
    if shards:
        values = values * steps_of(own_key, shape, shards, -0.22, 0.18)
    return jnp.clip(values, -most, most).astype(held_as)


def setup_inputs(seed: int = 0) -> dict:
    streams_of = jax.random.split(jax.random.key(seed), 9)
    tokens = scatter_about(streams_of[0], (NLAT, NLON, D), 1.0, 6.0, ((0, 4), (1, 8)))
    norm_gain = jnp.clip(1.0 + 0.18 * jax.random.normal(streams_of[1], (D,), jnp.float32), 0.1, 1.9)
    inproj_weight = draw_inproj_weight(jax.random.fold_in(streams_of[8], 71), 0)
    outproj_weight = scatter_about(streams_of[3], (HEADS * HD, D), (HEADS * HD) ** -0.5, 0.3125, ((0, 4),))
    merge_gain = jnp.clip(1.0 + 0.18 * jax.random.normal(streams_of[4], (4 * D,), jnp.float32), 0.1, 1.9)
    merge_weight = scatter_about(streams_of[5], (4 * D, DM), (4 * D) ** -0.5, 0.109375, ((0, 4),))
    ocean_flags = touch_ends((jax.random.randint(streams_of[6], (NLAT // WIN, NLON // WIN), 0, 4) < 3).astype(jnp.int32), jax.random.fold_in(streams_of[6], 1), 0, 1)
    fold_partner = draw_fold_partner(jax.random.fold_in(streams_of[8], 71), 0)
    return {"tokens": tokens, "norm_gain": norm_gain, "inproj_weight": inproj_weight, "outproj_weight": outproj_weight, "merge_gain": merge_gain, "merge_weight": merge_weight, "ocean_flags": ocean_flags, "fold_partner": fold_partner}


epsilon = 1e-05

def layer_norm(values, norm_scale):
    center = values - lax.optimization_barrier(jnp.mean(values, axis=-1, keepdims=True))
    spread = lax.optimization_barrier(jnp.mean(center * center, axis=-1, keepdims=True))
    return center * lax.rsqrt(spread + epsilon) * norm_scale

def to_windows(region):
    down_count = region.shape[0] // WIN
    across = region.shape[1] // WIN
    channel = region.shape[2]
    tiled_view = region.reshape(down_count, WIN, across, WIN, channel).transpose(0, 2, 1, 3, 4)
    return tiled_view.reshape(down_count * across, WIN * WIN, channel)

def from_windows(windows, down_count, across):
    channel = windows.shape[-1]
    tiled_view = windows.reshape(down_count, across, WIN, WIN, channel).transpose(0, 2, 1, 3, 4)
    return tiled_view.reshape(down_count * WIN, across * WIN, channel)

def window_branch(window, in_weight, out_weight, norm_scale):
    head_width = HEADS * HD
    normed = layer_norm(window.astype(jnp.float32), norm_scale).astype(jnp.bfloat16)
    packed = jnp.dot(normed, in_weight, preferred_element_type=jnp.float32).astype(jnp.bfloat16)
    queries = packed[:, :head_width].reshape(-1, HEADS, HD).astype(jnp.float32)
    key_cols = packed[:, head_width:2 * head_width].reshape(-1, HEADS, HD).astype(jnp.float32)
    value_cols = packed[:, 2 * head_width:].reshape(-1, HEADS, HD).astype(jnp.float32)
    scores = jnp.einsum('qhd,khd->hqk', queries, key_cols) * HD ** (-0.5)
    highest = lax.optimization_barrier(jnp.max(scores, axis=-1, keepdims=True))
    lifted = jnp.exp(scores - highest)
    weights = (lifted / lax.optimization_barrier(jnp.sum(lifted, axis=-1, keepdims=True))).astype(jnp.bfloat16)
    mixed_heads = jnp.einsum('hqk,khd->qhd', weights.astype(jnp.float32), value_cols)
    mixed_heads = mixed_heads.reshape(-1, head_width).astype(jnp.bfloat16)
    return jnp.dot(mixed_heads, out_weight, preferred_element_type=jnp.float32)

def reference(tokens, norm_gain, inproj_weight, outproj_weight, merge_gain, merge_weight, ocean_flags, fold_partner):
    top_rows = (NLAT - 1 - jnp.arange(HALF)).astype(jnp.int32)
    fold_rows = tokens[top_rows][:, fold_partner.astype(jnp.int32)]
    extended = jnp.concatenate([tokens[HALF:], fold_rows], axis=0)

    def branch_of(window):
        return window_branch(window, inproj_weight, outproj_weight, norm_gain)

    def one_band(band_index):
        band = lax.dynamic_slice_in_dim(extended, band_index * WIN, WIN, 0)
        band = jnp.roll(band, -HALF, axis=1)
        flags = lax.dynamic_index_in_dim(ocean_flags, band_index, 0, keepdims=False)
        windows = to_windows(band)
        branch = jax.vmap(branch_of)(windows)
        kept = jnp.where(flags[:, None, None] > 0, branch, jnp.zeros_like(branch))
        attended = (windows.astype(jnp.float32) + kept).astype(jnp.bfloat16)
        attended = from_windows(attended, 1, NLON // WIN)
        quadrants = jnp.concatenate([attended[0::2, 0::2], attended[1::2, 0::2], attended[0::2, 1::2], attended[1::2, 1::2]], axis=-1)
        merge_normed = layer_norm(quadrants.reshape(-1, 4 * D).astype(jnp.float32), merge_gain).astype(jnp.bfloat16)
        result = jnp.dot(merge_normed, merge_weight, preferred_element_type=jnp.float32).astype(jnp.bfloat16)
        return result.reshape(HALF, NLON // 2, DM)
    merged = lax.map(one_band, jnp.arange(NLAT // WIN, dtype=jnp.int32))
    return merged.reshape(NLAT // 2, NLON // 2, DM)
```

```python
import functools
import math

import jax
import jax.numpy as jnp
from jax import lax
from jax.experimental import pallas as pl
from jax.experimental.pallas import tpu as pltpu
from jax.sharding import PartitionSpec as P

HEADS = 12
HD = 32
WIN = 16
HALF = WIN // 2
GROUP = 4
epsilon = 1e-05

MESH = pl.DeviceIdType.MESH


def kernel(
    spread,
    tokens,
    norm_gain,
    in_shard,
    out_shard,
    merge_gain,
    merge_shard,
    flags,
    partners,
    out,
    windows,
    mirror,
    corner,
    order,
    w_in,
    w_out,
    w_merge,
    packed_ref,
    mixed_ref,
    merge_in,
    local_sem,
    halo_send,
    halo_recv,
    w_local,
    w_send,
    w_recv,
):
    lat, lon = lax.axis_index("lat"), lax.axis_index("lon")
    n_lat, n_lon = lax.axis_size("lat"), lax.axis_size("lon")
    rows, width = tokens.shape[0], tokens.shape[3]
    head_width = HEADS * HD
    is_top = lat == n_lat - 1
    west, east = lax.rem(lon + n_lon - 1, n_lon), lax.rem(lon + 1, n_lon)
    south, north = lax.rem(lat + n_lat - 1, n_lat), lax.rem(lat + 1, n_lat)
    facing = n_lon - 1 - lon
    mate = lat + 1 - 2 * lax.rem(lat, 2)
    across = lax.rem(lat + 2, 4)
    across_mate = mate + across - lat
    side = lax.rem(lon, 2)
    beside = lon + 1 - 2 * side

    local = []

    def move(src, dst):
        copy = pltpu.make_async_copy(src, dst, local_sem.at[len(local)])
        copy.start()
        local.append(copy)

    move(tokens.at[pl.ds(HALF, WIN), 1], windows.at[0, 0])
    move(tokens.at[pl.ds(HALF, WIN), 2], windows.at[0, 1])
    move(tokens.at[pl.ds(HALF, WIN), 3], windows.at[1, 0])
    tail = rows - HALF
    for at, (w, h) in ((1, (2, 0)), (2, (2, 1)), (3, (3, 0))):
        move(tokens.at[pl.ds(tail, HALF), at], windows.at[w, h, pl.ds(0, HALF)])

    n_in, n_out, n_merge = in_shard.shape[0], out_shard.shape[0], merge_shard.shape[0]
    half_merge = n_merge // 2 if spread else n_merge
    items = [(in_shard, 0, n_in, w_in), (out_shard, 0, n_out, w_out), (merge_shard, 0, half_merge, w_merge)]
    if spread:
        items.append((merge_shard, half_merge, half_merge, w_merge))
    size_of = [n_in, n_out, n_merge, n_merge]

    def place(k, shard, first, count):
        _, row0, _, dst = items[k]
        start = shard * size_of[k] + row0 + first
        return dst.at[pl.ds(pl.multiple_of(start, 16), count), :]

    own = []
    for k, (src, row0, count, _) in enumerate(items):
        me = lat if spread else 0
        copy = pltpu.make_async_copy(src.at[pl.ds(row0, count), :], place(k, me, 0, count), w_local.at[k])
        copy.start()
        own.append(copy)

    peers = [
        (south, lon), (north, lon), (lat, west), (lat, east), (south, west), (north, east), (lat, facing),
    ]
    if spread:
        peers += [(mate, lon), (across, lon), (lat, beside)]
    barrier = pltpu.get_barrier_semaphore()
    for a, b in peers:
        pl.semaphore_signal(barrier, inc=1, device_id={"lat": a, "lon": b}, device_id_type=MESH)

    t = lax.broadcasted_iota(jnp.int32, order.shape, 0)
    s = lax.broadcasted_iota(jnp.int32, order.shape, 1)
    quad, i, j = t >> 6, (t >> 3) & 7, t & 7
    r, c = 2 * i + (quad & 1), 2 * j + (quad >> 1)
    order[...] = jnp.where(s == (c >> 3) * 128 + r * 8 + (c & 7), 1.0, 0.0).astype(jnp.bfloat16)

    pl.semaphore_wait(barrier, len(peers))

    def remote(src, dst, send, recv, a, b):
        return pltpu.make_async_remote_copy(
            src_ref=src, dst_ref=dst, send_sem=send, recv_sem=recv,
            device_id={"lat": a, "lon": b}, device_id_type=MESH,
        )

    def hop(k, step):
        _, row0, count, _ = items[k]
        half = count // 2
        near, far = side * half, (1 - side) * half
        send, recv = w_send.at[k, step], w_recv.at[k, step]
        src = items[k][0]
        if step == 0:
            return remote(src.at[pl.ds(row0, count), :], place(k, lat, 0, count), send, recv, mate, lon)
        if step == 1:
            first = pl.multiple_of(row0 + near, 16)
            return remote(src.at[pl.ds(first, half), :], place(k, lat, near, half), send, recv, across, lon)
        if step == 2:
            ref = place(k, across, near, half)
            return remote(ref, ref, send, recv, lat, beside)
        if step == 3:
            ref = place(k, across, near, half)
            return remote(ref, ref, send, recv, mate, lon)
        ref = place(k, across, far, half)
        return remote(ref, ref, send, recv, mate, lon)

    def halo(n):
        head = pl.ds(0, HALF)
        late = pl.ds(HALF, HALF)
        if n < 3:
            w, h = ((2, 0), (2, 1), (3, 0))[n]
            return remote(tokens.at[head, n + 1], windows.at[w, h, late], halo_send.at[n], halo_recv.at[n], south, lon)
        if n == 3:
            return remote(tokens.at[head, 0], windows.at[3, 1, late], halo_send.at[3], halo_recv.at[3], south, west)
        if n == 4:
            return remote(tokens.at[pl.ds(HALF, WIN), 0], windows.at[1, 1], halo_send.at[4], halo_recv.at[4], lat, west)
        if n == 5:
            return remote(tokens.at[pl.ds(tail, HALF), 0], windows.at[3, 1, head], halo_send.at[5], halo_recv.at[5], lat, west)
        if n == 6:
            return remote(tokens.at[pl.ds(tail, HALF)], mirror, halo_send.at[6], halo_recv.at[6], lat, facing)
        return remote(corner, windows.at[3, 1, late], halo_send.at[7], halo_recv.at[7], lat, west)

    if spread:
        hop(0, 1).start()
        hop(0, 0).start()
        hop(1, 1).start()
        hop(1, 0).start()
    halo(4).start()

    @pl.when(is_top)
    def _():
        halo(6).start()

    @pl.when(lat > 0)
    def _():
        for n in range(4):
            halo(n).start()

    halo(5).start()
    if spread:
        for k in (2, 3):
            hop(k, 1).start()
            hop(k, 0).start()

        def pass_on(k):
            hop(k, 1).wait_recv()
            hop(k, 2).start()
            hop(k, 3).start()

        def pass_far(k):
            hop(k, 2).wait_recv()
            hop(k, 4).start()

        def arrived(k):
            for step in (0, 3, 4):
                hop(k, step).wait_recv()

        pass_on(0)
        pass_on(1)
        pass_far(0)
        pass_far(1)
        own[0].wait()
        own[1].wait()
        arrived(0)
        arrived(1)
    else:
        own[0].wait()
        own[1].wait()

    lane = lax.broadcasted_iota(jnp.int32, (1, GROUP * HD), 1)
    ones = jnp.ones((WIN * WIN, GROUP * HD), jnp.bfloat16)

    def fold():
        halo(6).wait_recv()
        tt = lax.broadcasted_iota(jnp.int32, (WIN * WIN, WIN * WIN), 0)
        ss = lax.broadcasted_iota(jnp.int32, (WIN * WIN, WIN * WIN), 1)
        column = (tt >> 6) * HALF + (tt & 7)
        first = (n_lon - 1 - lon) * (4 * HALF)
        source = jnp.zeros_like(tt)
        for k in range(4 * HALF):
            source = jnp.where(column == k, partners[k] - first, source)
        source = source + (HALF - 1 - ((tt >> 3) & 7)) * (4 * HALF)
        pick = jnp.where(ss == source, 1.0, 0.0).astype(jnp.bfloat16)
        raw = mirror[...].astype(jnp.float32).reshape(WIN * WIN, width).astype(jnp.bfloat16)
        folded = jnp.dot(pick, raw, preferred_element_type=jnp.float32)
        part = folded.reshape(4, HALF, HALF, width).astype(jnp.bfloat16)
        corner[...] = part[0]
        windows[2, 0, pl.ds(HALF, HALF)] = part[1]
        windows[2, 1, pl.ds(HALF, HALF)] = part[2]
        windows[3, 0, pl.ds(HALF, HALF)] = part[3]
        halo(7).start()

    def body(w, carry):
        @pl.when(w == 0)
        def _():
            local[0].wait()
            local[1].wait()

        @pl.when(w == 1)
        def _():
            if spread:
                pass_on(2)
            local[2].wait()
            halo(4).wait_recv()

        @pl.when(w == 2)
        def _():
            if spread:
                pass_on(3)
                pass_far(2)
            local[3].wait()
            local[4].wait()

            @pl.when(is_top)
            def _():
                fold()

            @pl.when(lat < n_lat - 1)
            def _():
                halo(0).wait_recv()
                halo(1).wait_recv()

        @pl.when(w == 3)
        def _():
            if spread:
                pass_far(3)
            local[5].wait()
            halo(5).wait_recv()

            @pl.when(is_top)
            def _():
                halo(7).wait_recv()

            @pl.when(lat < n_lat - 1)
            def _():
                halo(2).wait_recv()
                halo(3).wait_recv()

        raw = windows[w].astype(jnp.float32).reshape(WIN * WIN, width).astype(jnp.bfloat16)
        x = jnp.dot(order[...], raw, preferred_element_type=jnp.float32)
        center = x - jnp.sum(x, axis=-1, keepdims=True) * (1.0 / width)
        spread_of = jnp.sum(center * center, axis=-1, keepdims=True) * (1.0 / width)
        normed = (center * lax.rsqrt(spread_of + epsilon) * norm_gain[...]).astype(jnp.bfloat16)
        packed = jnp.dot(normed, w_in[...], preferred_element_type=jnp.float32)
        factor = HD ** (-0.5) * math.log2(math.e)
        packed_ref[:, :head_width] = (packed[:, :head_width] * factor).astype(jnp.bfloat16)
        packed_ref[:, head_width:] = packed[:, head_width:].astype(jnp.bfloat16)
        for g in range(HEADS // GROUP):
            at = g * GROUP * HD
            q = packed_ref[:, at : at + GROUP * HD]
            k = packed_ref[:, head_width + at : head_width + at + GROUP * HD]
            v = packed_ref[:, 2 * head_width + at : 2 * head_width + at + GROUP * HD]
            v = jnp.concatenate([v, ones], axis=1)
            mixed = jnp.zeros((WIN * WIN, GROUP * HD), jnp.float32)
            for h in range(GROUP):
                mine = (lane >= h * HD) & (lane < (h + 1) * HD)
                q_own = jnp.where(mine, q.astype(jnp.float32), 0.0).astype(jnp.bfloat16)
                scores = lax.dot_general(
                    q_own, k, (((1,), (1,)), ((), ())), preferred_element_type=jnp.float32
                )
                highest = jnp.max(scores, axis=-1, keepdims=True)
                lifted = jnp.exp2(scores - highest).astype(jnp.bfloat16)
                both = jnp.dot(lifted, v, preferred_element_type=jnp.float32)
                share = both[:, : GROUP * HD] / both[:, GROUP * HD :]
                mixed = jnp.where(mine, share, mixed)
            mixed_ref[:, at : at + GROUP * HD] = mixed.astype(jnp.bfloat16)
        branch = jnp.dot(mixed_ref[...], w_out[...], preferred_element_type=jnp.float32)
        kept = jnp.where(flags[w // 2, lax.rem(w, 2)] > 0, branch, 0.0)
        attended = (x + kept).astype(jnp.bfloat16).astype(jnp.float32)
        count = WIN * WIN // 4
        quads = [attended[n * count : (n + 1) * count] for n in range(4)]
        total = sum(jnp.sum(quad, axis=-1, keepdims=True) for quad in quads)
        mean = total * (1.0 / (4 * width))
        quads = [quad - mean for quad in quads]
        square = sum(jnp.sum(quad * quad, axis=-1, keepdims=True) for quad in quads)
        inverse = lax.rsqrt(square * (1.0 / (4 * width)) + epsilon)
        for n, quad in enumerate(quads):
            value = quad * inverse * merge_gain[n]
            merge_in[n, pl.ds(pl.multiple_of(w * count, count), count), :] = value.astype(jnp.bfloat16)
        return carry

    lax.fori_loop(0, 4, body, 0)

    def product(shard):
        weight = w_merge[pl.ds(pl.multiple_of(shard * width, width), width), :]
        return jnp.dot(merge_in[shard], weight, preferred_element_type=jnp.float32)

    if spread:
        own[2].wait()
        own[3].wait()
        total = product(lat)
        hop(2, 0).wait_recv()
        hop(3, 0).wait_recv()
        total = total + product(mate)
        total = total + product(across)
        for k in (2, 3):
            hop(k, 3).wait_recv()
            hop(k, 4).wait_recv()
        total = total + product(across_mate)
    else:
        own[2].wait()
        total = sum(product(n) for n in range(4))
    count = WIN * WIN // 4
    for w in range(4):
        piece = total[w * count : (w + 1) * count].reshape(HALF, HALF, total.shape[1])
        out[w // 2, :, w % 2] = piece.astype(out.dtype)

    if spread:
        for k in range(4):
            for step in range(5):
                hop(k, step).wait_send()
    halo(4).wait_send()
    halo(5).wait_send()

    @pl.when(is_top)
    def _():
        halo(6).wait_send()
        halo(7).wait_send()

    @pl.when(lat > 0)
    def _():
        for n in range(4):
            halo(n).wait_send()


def per_device(
    tokens, norm_gain, inproj_weight, outproj_weight, merge_gain, merge_weight, ocean_flags, fold_partner
):
    height, breadth, width = tokens.shape
    n_lat = lax.axis_size("lat")
    spread = (
        n_lat == 4
        and merge_weight.shape[0] == width
        and all(w.shape[0] % 32 == 0 for w in (inproj_weight, outproj_weight))
    )
    if not spread:
        inproj_weight, outproj_weight, merge_weight = (
            lax.all_gather(w, "lat", axis=0, tiled=True) for w in (inproj_weight, outproj_weight, merge_weight)
        )
    tall = n_lat if spread else 1
    in_rows, packed_width = inproj_weight.shape[0] * tall, inproj_weight.shape[1]
    out_rows = outproj_weight.shape[0] * tall
    merge_rows, merge_width = merge_weight.shape[0] * tall, merge_weight.shape[1]
    square = WIN * WIN
    vmem = pl.BlockSpec(memory_space=pltpu.VMEM)
    smem = pl.BlockSpec(memory_space=pltpu.SMEM)
    hbm = pl.BlockSpec(memory_space=pl.ANY)
    bf16 = jnp.bfloat16
    merged = pl.pallas_call(
        functools.partial(kernel, spread),
        out_shape=jax.ShapeDtypeStruct((2, HALF, 2, HALF, merge_width), bf16),
        in_specs=[hbm, vmem, hbm, hbm, vmem, hbm, smem, smem],
        out_specs=vmem,
        scratch_shapes=[
            pltpu.VMEM((4, 2, WIN, HALF, width), bf16),
            pltpu.VMEM((HALF, 4, HALF, width), bf16),
            pltpu.VMEM((HALF, HALF, width), bf16),
            pltpu.VMEM((square, square), bf16),
            pltpu.VMEM((in_rows, packed_width), bf16),
            pltpu.VMEM((out_rows, width), bf16),
            pltpu.VMEM((merge_rows, merge_width), bf16),
            pltpu.VMEM((square, packed_width), bf16),
            pltpu.VMEM((square, out_rows), bf16),
            pltpu.VMEM((4, square, width), bf16),
            pltpu.SemaphoreType.DMA((6,)),
            pltpu.SemaphoreType.DMA((8,)),
            pltpu.SemaphoreType.DMA((8,)),
            pltpu.SemaphoreType.DMA((4,)),
            pltpu.SemaphoreType.DMA((4, 5)),
            pltpu.SemaphoreType.DMA((4, 5)),
        ],
        compiler_params=pltpu.CompilerParams(
            collective_id=0, has_side_effects=True, vmem_limit_bytes=48 * 1024 * 1024
        ),
        name="window_attention_merge",
    )(
        tokens.reshape(height, breadth // HALF, HALF, width),
        norm_gain.reshape(1, width),
        inproj_weight,
        outproj_weight,
        merge_gain.reshape(4, 1, width),
        merge_weight,
        ocean_flags,
        fold_partner,
    )
    return merged.reshape(height // 2, breadth // 2, merge_width)


def solution(mesh):
    placed = (
        P("lat", "lon", None),
        P(),
        P("lat", None),
        P("lat", None),
        P(),
        P("lat", None),
        P("lat", "lon"),
        P("lon"),
    )
    return jax.shard_map(
        per_device, mesh=mesh, in_specs=placed, out_specs=P("lat", "lon", None), check_vma=False
    )
```

```python
import functools
import math

import jax
import jax.numpy as jnp
from jax import lax
from jax.experimental import pallas as pl
from jax.experimental.pallas import tpu as pltpu
from jax.sharding import PartitionSpec as P

HEADS = 12
HD = 32
WIN = 16
HALF = WIN // 2
CHUNKS = 4
GROUP = 4
epsilon = 1e-05

MESH = pl.DeviceIdType.MESH


def kernel(
    spread,
    tokens,
    norm_gain,
    in_shard,
    out_shard,
    merge_gain,
    merge_shard,
    flags,
    partners,
    out,
    windows,
    mirror,
    corner,
    order,
    w_in,
    w_out,
    w_merge,
    packed_ref,
    mixed_ref,
    merge_in,
    local_sem,
    halo_send,
    halo_recv,
    w_local,
    w_send,
    w_recv,
):
    lat, lon = lax.axis_index("lat"), lax.axis_index("lon")
    n_lat, n_lon = lax.axis_size("lat"), lax.axis_size("lon")
    rows, width = tokens.shape[0], tokens.shape[3]
    head_width = HEADS * HD
    is_top = lat == n_lat - 1
    west, east = lax.rem(lon + n_lon - 1, n_lon), lax.rem(lon + 1, n_lon)
    south, north = lax.rem(lat + n_lat - 1, n_lat), lax.rem(lat + 1, n_lat)
    facing = n_lon - 1 - lon
    mate = lat + 1 - 2 * lax.rem(lat, 2)
    across = lax.rem(lat + 2, 4)
    across_mate = mate + across - lat
    odd, odd_pair = lax.rem(lon, 2), lax.rem(lon // 2, 2)
    side = lax.rem(odd + odd_pair, 2)
    beside = lon + 1 - 2 * odd
    behind = lon + 2 - 4 * odd_pair

    local = []

    def move(src, dst):
        copy = pltpu.make_async_copy(src, dst, local_sem.at[len(local)])
        copy.start()
        local.append(copy)

    move(tokens.at[pl.ds(HALF, WIN), 1], windows.at[0, 0])
    move(tokens.at[pl.ds(HALF, WIN), 2], windows.at[0, 1])
    move(tokens.at[pl.ds(HALF, WIN), 3], windows.at[1, 0])
    tail = rows - HALF
    for at, (w, h) in ((1, (2, 0)), (2, (2, 1)), (3, (3, 0))):
        move(tokens.at[pl.ds(tail, HALF), at], windows.at[w, h, pl.ds(0, HALF)])

    n_in, n_out, n_merge = in_shard.shape[0], out_shard.shape[0], merge_shard.shape[0]
    chunks = CHUNKS if spread else 1
    items = [(in_shard, 0, n_in, w_in), (out_shard, 0, n_out, w_out)]
    for n in range(chunks):
        items.append((merge_shard, n * (n_merge // chunks), n_merge // chunks, w_merge))
    size_of = [n_in, n_out] + [n_merge] * chunks
    merge_items = range(2, 2 + chunks)

    def place(k, shard, first, count):
        _, row0, _, dst = items[k]
        start = shard * size_of[k] + row0 + first
        return dst.at[pl.ds(pl.multiple_of(start, 16), count), :]

    own = []
    for k, (src, row0, count, _) in enumerate(items):
        me = lat if spread else 0
        copy = pltpu.make_async_copy(src.at[pl.ds(row0, count), :], place(k, me, 0, count), w_local.at[k])
        copy.start()
        own.append(copy)

    peers = [
        (south, lon), (north, lon), (lat, west), (lat, east), (south, west), (north, east), (lat, facing),
    ]
    if spread:
        peers += [(mate, lon), (across, lon), (lat, beside), (lat, behind)]
    barrier = pltpu.get_barrier_semaphore()
    for a, b in peers:
        pl.semaphore_signal(barrier, inc=1, device_id={"lat": a, "lon": b}, device_id_type=MESH)

    t = lax.broadcasted_iota(jnp.int32, order.shape, 0)
    s = lax.broadcasted_iota(jnp.int32, order.shape, 1)
    quad, i, j = t >> 6, (t >> 3) & 7, t & 7
    r, c = 2 * i + (quad & 1), 2 * j + (quad >> 1)
    order[...] = jnp.where(s == (c >> 3) * 128 + r * 8 + (c & 7), 1.0, 0.0).astype(jnp.bfloat16)

    pl.semaphore_wait(barrier, len(peers))

    def remote(src, dst, send, recv, a, b):
        return pltpu.make_async_remote_copy(
            src_ref=src, dst_ref=dst, send_sem=send, recv_sem=recv,
            device_id={"lat": a, "lon": b}, device_id_type=MESH,
        )

    def hop(k, step):
        _, row0, count, _ = items[k]
        half = count // 2
        near, far = side * half, (1 - side) * half
        send, recv = w_send.at[k, step], w_recv.at[k, step]
        src = items[k][0]
        if step == 0:
            return remote(src.at[pl.ds(row0, count), :], place(k, lat, 0, count), send, recv, mate, lon)
        if step == 1:
            first = pl.multiple_of(row0 + near, 16)
            return remote(src.at[pl.ds(first, half), :], place(k, lat, near, half), send, recv, across, lon)
        part = -(-half // 32) * 16
        if step == 2:
            ref = place(k, across, near, part)
            return remote(ref, ref, send, recv, lat, beside)
        if step == 3:
            ref = place(k, across, near + part, half - part)
            return remote(ref, ref, send, recv, lat, behind)
        if step == 4:
            ref = place(k, across, near, half)
        elif step == 5:
            ref = place(k, across, far, part)
        else:
            ref = place(k, across, far + part, half - part)
        return remote(ref, ref, send, recv, mate, lon)

    def halo(n):
        head = pl.ds(0, HALF)
        late = pl.ds(HALF, HALF)
        if n < 3:
            w, h = ((2, 0), (2, 1), (3, 0))[n]
            return remote(tokens.at[head, n + 1], windows.at[w, h, late], halo_send.at[n], halo_recv.at[n], south, lon)
        if n == 3:
            return remote(tokens.at[head, 0], windows.at[3, 1, late], halo_send.at[3], halo_recv.at[3], south, west)
        if n == 4:
            return remote(tokens.at[pl.ds(HALF, WIN), 0], windows.at[1, 1], halo_send.at[4], halo_recv.at[4], lat, west)
        if n == 5:
            return remote(tokens.at[pl.ds(tail, HALF), 0], windows.at[3, 1, head], halo_send.at[5], halo_recv.at[5], lat, west)
        if n == 6:
            return remote(tokens.at[pl.ds(tail, HALF)], mirror, halo_send.at[6], halo_recv.at[6], lat, facing)
        return remote(corner, windows.at[3, 1, late], halo_send.at[7], halo_recv.at[7], lat, west)

    if spread:
        hop(0, 1).start()
        hop(0, 0).start()
        hop(1, 1).start()
        hop(1, 0).start()
    halo(4).start()

    @pl.when(is_top)
    def _():
        halo(6).start()

    @pl.when(lat > 0)
    def _():
        for n in range(4):
            halo(n).start()

    if spread:
        for k in merge_items:
            hop(k, 1).start()
            hop(k, 0).start()

        def pass_on(k):
            hop(k, 1).wait_recv()
            for step in (2, 3, 4):
                hop(k, step).start()

        def pass_far(k):
            for step in (2, 3):
                hop(k, step).wait_recv()
                hop(k, step + 3).start()

        def arrived(k):
            for step in (0, 4, 5, 6):
                hop(k, step).wait_recv()

        pass_on(0)
        pass_on(1)
        halo(5).start()
        pass_far(0)
        pass_far(1)
        own[0].wait()
        own[1].wait()
        arrived(0)
        arrived(1)
    else:
        halo(5).start()
        own[0].wait()
        own[1].wait()

    lane = lax.broadcasted_iota(jnp.int32, (1, GROUP * HD), 1)
    ones = jnp.ones((WIN * WIN, GROUP * HD), jnp.bfloat16)

    def fold():
        halo(6).wait_recv()
        tt = lax.broadcasted_iota(jnp.int32, (WIN * WIN, WIN * WIN), 0)
        ss = lax.broadcasted_iota(jnp.int32, (WIN * WIN, WIN * WIN), 1)
        column = (tt >> 6) * HALF + (tt & 7)
        first = (n_lon - 1 - lon) * (4 * HALF)
        source = jnp.zeros_like(tt)
        for k in range(4 * HALF):
            source = jnp.where(column == k, partners[k] - first, source)
        source = source + (HALF - 1 - ((tt >> 3) & 7)) * (4 * HALF)
        pick = jnp.where(ss == source, 1.0, 0.0).astype(jnp.bfloat16)
        raw = mirror[...].astype(jnp.float32).reshape(WIN * WIN, width).astype(jnp.bfloat16)
        folded = jnp.dot(pick, raw, preferred_element_type=jnp.float32)
        part = folded.reshape(4, HALF, HALF, width).astype(jnp.bfloat16)
        corner[...] = part[0]
        windows[2, 0, pl.ds(HALF, HALF)] = part[1]
        windows[2, 1, pl.ds(HALF, HALF)] = part[2]
        windows[3, 0, pl.ds(HALF, HALF)] = part[3]
        halo(7).start()

    def body(w, carry):
        @pl.when(w == 0)
        def _():
            local[0].wait()
            local[1].wait()

        @pl.when(w == 1)
        def _():
            if spread:
                pass_on(2)
            local[2].wait()
            halo(4).wait_recv()

        @pl.when(w == 2)
        def _():
            if spread:
                pass_on(3)
                pass_far(2)
            local[3].wait()
            local[4].wait()

            @pl.when(is_top)
            def _():
                fold()

            @pl.when(lat < n_lat - 1)
            def _():
                halo(0).wait_recv()
                halo(1).wait_recv()

        @pl.when(w == 3)
        def _():
            if spread:
                pass_on(4)
                pass_far(3)
            local[5].wait()
            halo(5).wait_recv()

            @pl.when(is_top)
            def _():
                halo(7).wait_recv()

            @pl.when(lat < n_lat - 1)
            def _():
                halo(2).wait_recv()
                halo(3).wait_recv()

        raw = windows[w].astype(jnp.float32).reshape(WIN * WIN, width).astype(jnp.bfloat16)
        x = jnp.dot(order[...], raw, preferred_element_type=jnp.float32)
        center = x - jnp.sum(x, axis=-1, keepdims=True) * (1.0 / width)
        spread_of = jnp.sum(center * center, axis=-1, keepdims=True) * (1.0 / width)
        normed = (center * lax.rsqrt(spread_of + epsilon) * norm_gain[...]).astype(jnp.bfloat16)
        packed = jnp.dot(normed, w_in[...], preferred_element_type=jnp.float32)
        factor = HD ** (-0.5) * math.log2(math.e)
        packed_ref[:, :head_width] = (packed[:, :head_width] * factor).astype(jnp.bfloat16)
        packed_ref[:, head_width:] = packed[:, head_width:].astype(jnp.bfloat16)
        for g in range(HEADS // GROUP):
            at = g * GROUP * HD
            q = packed_ref[:, at : at + GROUP * HD]
            k = packed_ref[:, head_width + at : head_width + at + GROUP * HD]
            v = packed_ref[:, 2 * head_width + at : 2 * head_width + at + GROUP * HD]
            v = jnp.concatenate([v, ones], axis=1)
            mixed = jnp.zeros((WIN * WIN, GROUP * HD), jnp.float32)
            for h in range(GROUP):
                mine = (lane >= h * HD) & (lane < (h + 1) * HD)
                q_own = jnp.where(mine, q.astype(jnp.float32), 0.0).astype(jnp.bfloat16)
                scores = lax.dot_general(
                    q_own, k, (((1,), (1,)), ((), ())), preferred_element_type=jnp.float32
                )
                highest = jnp.max(scores, axis=-1, keepdims=True)
                lifted = jnp.exp2(scores - highest).astype(jnp.bfloat16)
                both = jnp.dot(lifted, v, preferred_element_type=jnp.float32)
                share = both[:, : GROUP * HD] / both[:, GROUP * HD :]
                mixed = jnp.where(mine, share, mixed)
            mixed_ref[:, at : at + GROUP * HD] = mixed.astype(jnp.bfloat16)
        branch = jnp.dot(mixed_ref[...], w_out[...], preferred_element_type=jnp.float32)
        kept = jnp.where(flags[w // 2, lax.rem(w, 2)] > 0, branch, 0.0)
        attended = (x + kept).astype(jnp.bfloat16).astype(jnp.float32)
        count = WIN * WIN // 4
        quads = [attended[n * count : (n + 1) * count] for n in range(4)]
        total = sum(jnp.sum(quad, axis=-1, keepdims=True) for quad in quads)
        mean = total * (1.0 / (4 * width))
        quads = [quad - mean for quad in quads]
        square = sum(jnp.sum(quad * quad, axis=-1, keepdims=True) for quad in quads)
        inverse = lax.rsqrt(square * (1.0 / (4 * width)) + epsilon)
        for n, quad in enumerate(quads):
            value = quad * inverse * merge_gain[n]
            merge_in[n, pl.ds(pl.multiple_of(w * count, count), count), :] = value.astype(jnp.bfloat16)
        return carry

    lax.fori_loop(0, 4, body, 0)

    def product(shard):
        weight = w_merge[pl.ds(pl.multiple_of(shard * width, width), width), :]
        return jnp.dot(merge_in[shard], weight, preferred_element_type=jnp.float32)

    for k in merge_items:
        own[k].wait()
    if spread:
        pass_on(5)
        pass_far(4)
        total = product(lat)
        pass_far(5)
        for k in merge_items:
            hop(k, 0).wait_recv()
        total = total + product(mate)
        total = total + product(across)
        for k in merge_items:
            for step in (4, 5, 6):
                hop(k, step).wait_recv()
        total = total + product(across_mate)
    else:
        total = sum(product(n) for n in range(4))
    count = WIN * WIN // 4
    for w in range(4):
        piece = total[w * count : (w + 1) * count].reshape(HALF, HALF, total.shape[1])
        out[w // 2, :, w % 2] = piece.astype(out.dtype)

    if spread:
        for k in range(len(items)):
            for step in range(7):
                hop(k, step).wait_send()
    halo(4).wait_send()
    halo(5).wait_send()

    @pl.when(is_top)
    def _():
        halo(6).wait_send()
        halo(7).wait_send()

    @pl.when(lat > 0)
    def _():
        for n in range(4):
            halo(n).wait_send()


def per_device(
    tokens, norm_gain, inproj_weight, outproj_weight, merge_gain, merge_weight, ocean_flags, fold_partner
):
    height, breadth, width = tokens.shape
    n_lat = lax.axis_size("lat")
    spread = (
        n_lat == 4
        and lax.axis_size("lon") % 4 == 0
        and merge_weight.shape[0] == width
        and all(w.shape[0] % 32 == 0 for w in (inproj_weight, outproj_weight))
        and width % (64 * CHUNKS) == 0
    )
    if not spread:
        inproj_weight, outproj_weight, merge_weight = (
            lax.all_gather(w, "lat", axis=0, tiled=True) for w in (inproj_weight, outproj_weight, merge_weight)
        )
    tall = n_lat if spread else 1
    in_rows, packed_width = inproj_weight.shape[0] * tall, inproj_weight.shape[1]
    out_rows = outproj_weight.shape[0] * tall
    merge_rows, merge_width = merge_weight.shape[0] * tall, merge_weight.shape[1]
    square = WIN * WIN
    vmem = pl.BlockSpec(memory_space=pltpu.VMEM)
    smem = pl.BlockSpec(memory_space=pltpu.SMEM)
    hbm = pl.BlockSpec(memory_space=pl.ANY)
    bf16 = jnp.bfloat16
    merged = pl.pallas_call(
        functools.partial(kernel, spread),
        out_shape=jax.ShapeDtypeStruct((2, HALF, 2, HALF, merge_width), bf16),
        in_specs=[hbm, vmem, hbm, hbm, vmem, hbm, smem, smem],
        out_specs=vmem,
        scratch_shapes=[
            pltpu.VMEM((4, 2, WIN, HALF, width), bf16),
            pltpu.VMEM((HALF, 4, HALF, width), bf16),
            pltpu.VMEM((HALF, HALF, width), bf16),
            pltpu.VMEM((square, square), bf16),
            pltpu.VMEM((in_rows, packed_width), bf16),
            pltpu.VMEM((out_rows, width), bf16),
            pltpu.VMEM((merge_rows, merge_width), bf16),
            pltpu.VMEM((square, packed_width), bf16),
            pltpu.VMEM((square, out_rows), bf16),
            pltpu.VMEM((4, square, width), bf16),
            pltpu.SemaphoreType.DMA((6,)),
            pltpu.SemaphoreType.DMA((8,)),
            pltpu.SemaphoreType.DMA((8,)),
            pltpu.SemaphoreType.DMA((2 + CHUNKS,)),
            pltpu.SemaphoreType.DMA((2 + CHUNKS, 7)),
            pltpu.SemaphoreType.DMA((2 + CHUNKS, 7)),
        ],
        compiler_params=pltpu.CompilerParams(
            collective_id=0, has_side_effects=True, vmem_limit_bytes=67043328
        ),
        name="window_attention_merge",
    )(
        tokens.reshape(height, breadth // HALF, HALF, width),
        norm_gain.reshape(1, width),
        inproj_weight,
        outproj_weight,
        merge_gain.reshape(4, 1, width),
        merge_weight,
        ocean_flags,
        fold_partner,
    )
    return merged.reshape(height // 2, breadth // 2, merge_width)


def solution(mesh):
    placed = (
        P("lat", "lon", None),
        P(),
        P("lat", None),
        P("lat", None),
        P(),
        P("lat", None),
        P("lat", "lon"),
        P("lon"),
    )
    return jax.shard_map(
        per_device, mesh=mesh, in_specs=placed, out_specs=P("lat", "lon", None), check_vma=False
    )
```
